768 devices in a mesh: gx: 64 (over z_lo, y, core), gy: 12 (over x, z_hi).
Axes of the slice: x: 4, y: 8, z: 12 (z_hi: 3, z_lo: 4; z = z_hi * 4 + z_lo), core: 2. Of those that a mesh axis runs over, the one named last changes fastest.
Arguments:
- load: float32 [64, 12, 96, 896], P('gx', 'gy'), may hold values from -80 to 80
- dual_operator: bfloat16 [64, 12, 896, 896], P('gx', 'gy'), may hold values from -1 to 2
- dirichlet: bfloat16 [64, 12, 896, 896], P('gx', 'gy'), may hold values from -1 to 2
- modes: bfloat16 [64, 12, 12, 896], P('gx', 'gy'), may hold values from -1 to 1
- coarse_inverse: float32 [64, 144, 12, 768], P('gx', None, 'gy'), may hold values from -1 to 2, as said below
- face_counts: int32 [64, 12, 4], P('gx', 'gy'), may hold values from 0 to 224, as said below
- partners: int32 [64, 12, 4, 224], P('gx', 'gy'), may hold values from 0 to 223, as said below
Outputs:
- multipliers: float32 [64, 12, 96, 896], P('gx', 'gy')
- residual: float32 [64, 12, 96, 896], P('gx', 'gy')
The draws below stay inside these ranges and needn't reach their ends.
Inputs may be any that keep to these rules, and one draw needn't show every extreme that they name: `face_counts`: the two faces of one interface have equal counts; faces on the grid's outer boundary have 0; every other face has at least half of 224; some face has exactly 224. `partners`: each face's list is a permutation of the slots that maps the live slots onto the live slots of the neighbour's facing face; the facing face's list is its inverse. `coarse_inverse`: the coarse inverse is symmetric: the entry of coefficients u, v equals that of v, u.
All inputs are finite; a program needn't handle non-finite values.
Results may differ from the reference program's by a relative error of at most 0.00365.
The reference program's roundings to bfloat16 on the way count: a program that leaves them out, or rounds other values in their place, can miss the bound.
Values may be sent and summed in bfloat16 or wider, within the bound.
A program may use at most 64 MiB of HBM per device.

```python
import jax
import jax.numpy as jnp
from jax import lax

FACE_SLOTS = 224
MULTIPLIERS = 896
LOAD_COLUMNS = 96
COARSE_MODES = 12
ITERATIONS = 2
SUBDOMAIN_ROWS = 64
SUBDOMAIN_COLS = 12
COARSE_SIZE = 9216


def clipped_noise(noise_key, shape):
    return jnp.clip(jax.random.normal(noise_key, shape, jnp.float32), -4.0, 4.0)


def coarse_basis(key):
    basis_key = jax.random.fold_in(key, 21)
    random_part = clipped_noise(basis_key, (SUBDOMAIN_ROWS, SUBDOMAIN_COLS, COARSE_MODES, MULTIPLIERS))
    return (random_part / jnp.sqrt(jnp.float32(MULTIPLIERS))).astype(jnp.bfloat16)


def draw_modes(key, part):
    return coarse_basis(key)


def draw_load(key, part):
    mode_rows = coarse_basis(key).astype(jnp.float32)
    weights = 3.0 * clipped_noise(jax.random.fold_in(key, 22), (SUBDOMAIN_ROWS, SUBDOMAIN_COLS, LOAD_COLUMNS, COARSE_MODES))
    random_part = clipped_noise(jax.random.fold_in(key, 23), (SUBDOMAIN_ROWS, SUBDOMAIN_COLS, LOAD_COLUMNS, MULTIPLIERS))
    return random_part + jnp.einsum('abrk,abkm->abrm', weights, mode_rows)


def dense_operator(key, salt_value):
    salted = jax.random.fold_in(key, salt_value)
    diag_key, noise_key = jax.random.split(salted)
    diagonal = jax.random.uniform(diag_key, (SUBDOMAIN_ROWS, SUBDOMAIN_COLS, MULTIPLIERS), jnp.float32, 0.6, 1.4)
    row_keys = jax.random.split(noise_key, SUBDOMAIN_ROWS)
    spread = 0.25 / jnp.sqrt(jnp.float32(2 * MULTIPLIERS))
    identity = jnp.eye(MULTIPLIERS, dtype=jnp.float32)

    def one_row(row_inputs):
        row_key, row_diagonal = row_inputs
        random_part = clipped_noise(row_key, (SUBDOMAIN_COLS, MULTIPLIERS, MULTIPLIERS))
        symmetric = (random_part + jnp.swapaxes(random_part, 1, 2)) * spread
        return (symmetric + row_diagonal[:, :, None] * identity).astype(jnp.bfloat16)
    return lax.map(one_row, (row_keys, diagonal))


def draw_dual_operator(key, part):
    return dense_operator(key, 31)


def draw_dirichlet(key, part):
    return dense_operator(key, 32)


def draw_coarse_inverse(key, part):
    salted = jax.random.fold_in(key, 33)
    diag_key, noise_key = jax.random.split(salted)
    diagonal = jax.random.uniform(diag_key, (COARSE_SIZE,), jnp.float32, 0.6, 1.4)
    random_part = clipped_noise(noise_key, (COARSE_SIZE, COARSE_SIZE))
    spread = 0.25 / jnp.sqrt(jnp.float32(2 * COARSE_SIZE))
    symmetric = (random_part + random_part.T) * spread + jnp.diag(diagonal)
    shaped = symmetric.reshape(SUBDOMAIN_ROWS, SUBDOMAIN_COLS, COARSE_MODES, SUBDOMAIN_ROWS, SUBDOMAIN_COLS, COARSE_MODES)
    return jnp.transpose(shaped, (0, 1, 2, 4, 3, 5)).reshape(SUBDOMAIN_ROWS, SUBDOMAIN_COLS * COARSE_MODES, SUBDOMAIN_COLS, SUBDOMAIN_ROWS * COARSE_MODES)


def interface_layout(key):
    salted = jax.random.fold_in(key, 41)
    keys_all = jax.random.split(salted, 6)
    grid_shape = (SUBDOMAIN_ROWS, SUBDOMAIN_COLS)
    lowest = FACE_SLOTS // 2
    count_x = jax.random.randint(keys_all[0], grid_shape, lowest, FACE_SLOTS + 1)
    count_y = jax.random.randint(keys_all[1], grid_shape, lowest, FACE_SLOTS + 1)
    row_index = lax.broadcasted_iota(jnp.int32, grid_shape, 0)
    col_index = lax.broadcasted_iota(jnp.int32, grid_shape, 1)
    full_row = jax.random.randint(keys_all[2], (), 0, SUBDOMAIN_ROWS - 1)
    full_col = jax.random.randint(keys_all[3], (), 0, SUBDOMAIN_COLS)
    count_x = jnp.where((row_index == full_row) & (col_index == full_col), FACE_SLOTS, count_x)
    count_x = jnp.where(row_index < SUBDOMAIN_ROWS - 1, count_x, 0).astype(jnp.int32)
    count_y = jnp.where(col_index < SUBDOMAIN_COLS - 1, count_y, 0).astype(jnp.int32)
    slot_index = lax.broadcasted_iota(jnp.int32, grid_shape + (FACE_SLOTS,), 2)

    def orders(order_key, live_counts):
        random_ranks = jax.random.randint(order_key, grid_shape + (FACE_SLOTS,), 0, 1 << 20)
        dead_flag = (slot_index >= live_counts[:, :, None]).astype(jnp.int32)
        scores = random_ranks * FACE_SLOTS + slot_index + dead_flag * ((1 << 20) * FACE_SLOTS)
        forward = jnp.argsort(scores, axis=2).astype(jnp.int32)
        backward = jnp.argsort(forward, axis=2).astype(jnp.int32)
        return (forward, backward)
    forward_x, backward_x = orders(keys_all[4], count_x)
    forward_y, backward_y = orders(keys_all[5], count_y)
    zero_row = jnp.zeros((1, SUBDOMAIN_COLS), jnp.int32)
    zero_col = jnp.zeros((SUBDOMAIN_ROWS, 1), jnp.int32)
    west_count = jnp.concatenate([zero_row, count_x[:-1]], axis=0)
    south_count = jnp.concatenate([zero_col, count_y[:, :-1]], axis=1)
    counts = jnp.stack([west_count, count_x, south_count, count_y], axis=2).astype(jnp.int32)
    west_lists = jnp.concatenate([slot_index[:1], backward_x[:-1]], axis=0)
    south_lists = jnp.concatenate([slot_index[:, :1], backward_y[:, :-1]], axis=1)
    partner_lists = jnp.stack([west_lists, forward_x, south_lists, forward_y], axis=2).astype(jnp.int32)
    return (counts, partner_lists)


def draw_face_counts(key, part):
    counts, partner_lists = interface_layout(key)
    return counts


def draw_partners(key, part):
    counts, partner_lists = interface_layout(key)
    return partner_lists


def setup_inputs(seed: int = 0) -> dict:
    arg_keys = jax.random.split(jax.random.key(seed), 8)
    load = draw_load(jax.random.fold_in(arg_keys[7], 71), 0)
    dual_operator = draw_dual_operator(jax.random.fold_in(arg_keys[7], 71), 0)
    dirichlet = draw_dirichlet(jax.random.fold_in(arg_keys[7], 71), 0)
    modes = draw_modes(jax.random.fold_in(arg_keys[7], 71), 0)
    coarse_inverse = draw_coarse_inverse(jax.random.fold_in(arg_keys[7], 71), 0)
    face_counts = draw_face_counts(jax.random.fold_in(arg_keys[7], 71), 0)
    partners = draw_partners(jax.random.fold_in(arg_keys[7], 71), 0)
    return {"load": load, "dual_operator": dual_operator, "dirichlet": dirichlet, "modes": modes, "coarse_inverse": coarse_inverse, "face_counts": face_counts, "partners": partners}


precise = lax.Precision.HIGHEST
spectrum_low = 0.5
spectrum_high = 4.0


def chebyshev_coefficients(iteration_count):
    center = (spectrum_high + spectrum_low) / 2.0
    radius = (spectrum_high - spectrum_low) / 2.0
    center_ratio = center / radius
    factor_prev = 1.0 / center_ratio
    result = [(1.0 / center, 0.0)]
    for iteration in range(1, iteration_count):
        factor = 1.0 / (2.0 * center_ratio - factor_prev)
        result.append((2.0 * factor / radius, factor * factor_prev))
        factor_prev = factor
    return result


def live_mask(face_counts):
    positions = lax.broadcasted_iota(jnp.int32, (1, 1, 4, FACE_SLOTS), 3)
    live_slots = (positions < face_counts[:, :, :, None]).astype(jnp.float32)
    return live_slots.reshape(SUBDOMAIN_ROWS, SUBDOMAIN_COLS, 1, MULTIPLIERS)


def interface_sum(values, partners, live_slots):
    face_blocks = values.reshape(SUBDOMAIN_ROWS, SUBDOMAIN_COLS, LOAD_COLUMNS, 4, FACE_SLOTS)
    face_west = face_blocks[:, :, :, 0]
    face_east = face_blocks[:, :, :, 1]
    face_south = face_blocks[:, :, :, 2]
    face_north = face_blocks[:, :, :, 3]
    empty_row = jnp.zeros_like(face_west[:1])
    empty_col = jnp.zeros_like(face_west[:, :1])
    from_west = jnp.concatenate([empty_row, face_east[:-1]], axis=0)
    from_east = jnp.concatenate([face_west[1:], empty_row], axis=0)
    from_south = jnp.concatenate([empty_col, face_north[:, :-1]], axis=1)
    from_north = jnp.concatenate([face_south[:, 1:], empty_col], axis=1)
    incoming = jnp.stack([from_west, from_east, from_south, from_north], axis=3)
    gather_index = jnp.broadcast_to(partners[:, :, None], incoming.shape).astype(jnp.int32)
    matched = jnp.take_along_axis(incoming, gather_index, axis=4)
    return (values + matched.reshape(values.shape)) * live_slots


def coarse_solve(vector, mode_rows, inverse_full):
    coeffs = jnp.einsum("abrm,abkm->abrk", vector, mode_rows, precision=precise)
    flat_coeffs = jnp.transpose(coeffs, (0, 1, 3, 2)).reshape(COARSE_SIZE, LOAD_COLUMNS)
    solved = jnp.dot(inverse_full, flat_coeffs, precision=precise, preferred_element_type=jnp.float32)
    solved = jnp.transpose(solved.reshape(SUBDOMAIN_ROWS, SUBDOMAIN_COLS, COARSE_MODES, LOAD_COLUMNS), (0, 1, 3, 2))
    return jnp.einsum("abrk,abkm->abrm", solved, mode_rows, precision=precise)


def local_products(vector, matrices):
    def one_row(row_inputs):
        row_vectors, row_matrices = row_inputs
        rounded = row_vectors.astype(jnp.bfloat16)
        rounded = lax.optimization_barrier(rounded)
        widened = rounded.astype(jnp.float32)
        return jnp.einsum("brm,bmn->brn", widened, row_matrices.astype(jnp.float32))
    return lax.map(one_row, (vector, matrices))


def reference(load, dual_operator, dirichlet, modes, coarse_inverse, face_counts, partners):
    live_slots = live_mask(face_counts)
    mode_rows = modes.astype(jnp.float32)
    inverse_full = jnp.transpose(
        coarse_inverse.reshape(SUBDOMAIN_ROWS, SUBDOMAIN_COLS, COARSE_MODES, SUBDOMAIN_COLS, SUBDOMAIN_ROWS, COARSE_MODES),
        (0, 1, 2, 4, 3, 5)).reshape(COARSE_SIZE, COARSE_SIZE)

    def assemble(values):
        return interface_sum(values, partners, live_slots)

    def project(vector):
        return vector - assemble(coarse_solve(vector, mode_rows, inverse_full))

    gap_values = assemble(load)
    residual = project(gap_values)
    multipliers = jnp.zeros_like(load)
    direction = jnp.zeros_like(load)
    for alpha_step, beta_step in chebyshev_coefficients(ITERATIONS):
        preconditioned = project(assemble(local_products(residual, dirichlet)))
        direction = alpha_step * preconditioned + beta_step * direction
        multipliers = multipliers + direction
        residual = residual - project(assemble(local_products(direction, dual_operator)))
    return multipliers, residual
```

```python
import functools

import jax
import jax.numpy as jnp
from jax import lax
from jax.experimental import pallas as pl
from jax.experimental.pallas import tpu as pltpu
from jax.sharding import PartitionSpec as P

MESH = pl.DeviceIdType.MESH
F32 = jnp.float32
BF16 = jnp.bfloat16
ROUNDS = 5
spectrum_low = 0.5
spectrum_high = 4.0


def chebyshev_coefficients():
    center = (spectrum_high + spectrum_low) / 2.0
    radius = (spectrum_high - spectrum_low) / 2.0
    center_ratio = center / radius
    factor_prev = 1.0 / center_ratio
    result = [(1.0 / center, 0.0)]
    factor = 1.0 / (2.0 * center_ratio - factor_prev)
    result.append((2.0 * factor / radius, factor * factor_prev))
    return result


def halves(x):
    high = x.astype(BF16)
    return high, (x - high.astype(F32)).astype(BF16)


def thirds(x):
    high = x.astype(BF16)
    rest = x - high.astype(F32)
    mid = rest.astype(BF16)
    return high, mid, (rest - mid.astype(F32)).astype(BF16)


def mm(a, b):
    return jnp.dot(a, b, preferred_element_type=F32)


def dot_nt(a, b):
    return lax.dot_general(a, b, (((1,), (1,)), ((), ())), preferred_element_type=F32)


def dot_tn(a, b):
    return lax.dot_general(a, b, (((0,), (0,)), ((), ())), preferred_element_type=F32)


def kernel(
    nx, ny,
    slot_ref, load_ref, modes_ref, dual_hbm, dirichlet_hbm, inverse_hbm,
    mult_ref, res_ref,
    weights, inverse_raw, pick, mode_ext, mode_send, mode_recv,
    y_ref, v_ref, dir_ref, inv_high, inv_low,
    face_send, face_recv, part_send, part_recv, gathered,
    partial, scattered, solved_send, solved_recv,
    local_sem, mode_ssem, mode_rsem, face_ssem, face_rsem, part_ssem, part_rsem,
    gather_ssem, gather_rsem, relay_ssem, relay_rsem,
    scatter_ssem, scatter_rsem, solved_ssem, solved_rsem,
):
    loads, slots = load_ref.shape
    modes = modes_ref.shape[0]
    face = slots // 4
    face_pad = face_send.shape[2]
    padded = gathered.shape[3]
    lanes = gathered.shape[4]
    chips = nx // 2
    a = lax.axis_index("gx")
    b = lax.axis_index("gy")
    core = lax.rem(a, 2)
    chip = lax.div(a, 2)
    partner = a + 1 - 2 * core
    exists = (a > 0, a < nx - 1, b > 0, b < ny - 1)
    neighbours = ((a - 1, b), (a + 1, b), (a, b - 1), (a, b + 1))

    def remote(src, dst, ssem, rsem, device):
        return pltpu.make_async_remote_copy(
            src_ref=src, dst_ref=dst, send_sem=ssem, recv_sem=rsem,
            device_id=device, device_id_type=MESH)

    copies = (
        pltpu.make_async_copy(inverse_hbm, inverse_raw, local_sem.at[0]),
        pltpu.make_async_copy(dirichlet_hbm, weights.at[0], local_sem.at[1]),
        pltpu.make_async_copy(dual_hbm, weights.at[1], local_sem.at[2]),
    )
    for c in copies:
        c.start()

    barrier = pltpu.get_barrier_semaphore()

    def greet(device):
        pl.semaphore_signal(barrier, inc=1, device_id=device, device_id_type=MESH)

    @pl.loop(1, chips)
    def _(i):
        greet((2 * lax.rem(chip + i, chips) + core, b))

    @pl.loop(1, ny)
    def _(i):
        greet((a, lax.rem(b + i, ny)))

    for f in (0, 1):
        @pl.when(exists[f])
        def _(f=f):
            greet(neighbours[f])

    wide = modes_ref[...].astype(F32)
    mode_send[...] = jnp.zeros_like(mode_send)
    for f in range(4):
        mode_send[f, 0:modes, 0:face] = wide[:, f * face:(f + 1) * face]
    face_send[...] = jnp.zeros_like(face_send)
    part_send[...] = jnp.zeros_like(part_send)
    slot = slot_ref[...]
    live = (slot >= 0).astype(F32)
    for f in range(4):
        rows = lax.broadcasted_iota(jnp.int32, (face_pad, slots), 0) + f * face_pad
        pick[f] = (rows == slot).astype(F32).astype(BF16)
    own_modes = jnp.concatenate([wide * live, jnp.zeros((padded - modes, slots), F32)], axis=0)
    mode_ext[0:padded, :] = own_modes.astype(BF16)
    y_ref[...] = load_ref[...]

    pl.semaphore_wait(
        barrier, chips - 1 + ny - 1 + (a > 0).astype(jnp.int32) + (a < nx - 1).astype(jnp.int32))

    def mode_copy(f, g):
        return remote(mode_send.at[f], mode_recv.at[g], mode_ssem.at[f], mode_rsem.at[g], neighbours[f])

    for f in range(4):
        @pl.when(exists[f])
        def _(f=f):
            mode_copy(f, f ^ 1).start()

    copies[0].wait()
    raw_high, raw_low = halves(inverse_raw[...])
    out_row = lax.broadcasted_iota(jnp.int32, (ny * padded, ny * modes), 0)
    in_row = lax.broadcasted_iota(jnp.int32, (ny * padded, ny * modes), 1)
    place = lax.bitwise_and(out_row, padded - 1)
    row_pick = ((lax.shift_right_logical(out_row, 4) * modes + place == in_row) & (place < modes))
    row_pick = row_pick.astype(F32).astype(BF16)
    raw_high = mm(row_pick, raw_high).astype(BF16)
    raw_low = mm(row_pick, raw_low).astype(BF16)
    for p in range(2):
        in_col = lax.broadcasted_iota(jnp.int32, (nx * modes, chips * padded), 0)
        out_col = lax.broadcasted_iota(jnp.int32, (nx * modes, chips * padded), 1)
        place = lax.bitwise_and(out_col, padded - 1)
        source = (2 * lax.shift_right_logical(out_col, 4) + p) * modes + place
        col_pick = ((source == in_col) & (place < modes)).astype(F32).astype(BF16)
        inv_high[p] = mm(raw_high, col_pick).astype(BF16)
        inv_low[p] = mm(raw_low, col_pick).astype(BF16)
    copies[1].wait()
    copies[2].wait()

    for f in range(4):
        @pl.when(exists[f])
        def _(f=f):
            mode_copy(f, f).wait_recv()
        given = jnp.where(exists[f], mode_recv[f], 0.0).astype(BF16)
        mode_ext[(f + 1) * padded:(f + 2) * padded, :] = mm(given, pick[f]).astype(BF16)

    for f in range(4):
        @pl.when(exists[f])
        def _(f=f):
            mode_copy(f, f ^ 1).wait_send()

    used_row = lax.broadcasted_iota(jnp.int32, (padded, lanes), 0) < modes
    chebyshev = chebyshev_coefficients()

    def body(r, carry):
        def part_copy(f, g):
            return remote(part_send.at[f + 1, 0:modes], part_recv.at[r, g, 0:modes],
                          part_ssem.at[f], part_rsem.at[r, g], neighbours[f])

        def face_copy(f, g):
            return remote(face_send.at[f], face_recv.at[r, g],
                          face_ssem.at[f], face_rsem.at[r, g], neighbours[f])

        def solved_copy(f, g):
            return remote(solved_send.at[0:modes], solved_recv.at[r, g, 0:modes],
                          solved_ssem.at[f], solved_rsem.at[r, g], neighbours[f])

        def gather_copy(block, device):
            return remote(block, block, gather_ssem, gather_rsem.at[r], device)

        def relay_copy(p):
            block = gathered.at[r, p, :, 0:modes]
            return remote(block, block, relay_ssem, relay_rsem.at[r], (partner, b))

        def scatter_copy(src, dst, device):
            return remote(src, dst, scatter_ssem, scatter_rsem.at[r], device)

        y = y_ref[...]
        y_high, y_low = halves(y)
        parts = dot_nt(mode_ext[...], y_high) + dot_nt(mode_ext[...], y_low)
        for f in range(5):
            part_send[f, :, 0:loads] = parts[f * padded:(f + 1) * padded]
        for f in range(4):
            @pl.when(exists[f])
            def _(f=f):
                part_copy(f, f ^ 1).start()
        for f in range(4):
            face_send[f, :, 0:face] = y[:, f * face:(f + 1) * face]

        coeffs = part_send[0]
        for f in range(4):
            @pl.when(exists[f])
            def _(f=f):
                part_copy(f, f).wait_recv()
            coeffs = coeffs + jnp.where(exists[f], part_recv[r, f], 0.0)
        gathered[r, core, chip] = coeffs

        @pl.loop(1, chips)
        def _(i):
            gather_copy(gathered.at[r, core, chip, 0:modes],
                        (2 * lax.rem(chip + i, chips) + core, b)).start()

        for f in range(4):
            @pl.when(exists[f])
            def _(f=f):
                face_copy(f, f ^ 1).start()

        others = gathered.at[r, core, 0:chips - 1, 0:modes]
        gather_copy(others, (partner, b)).wait_recv()
        relay_copy(core).start()

        def coarse(p):
            values = jnp.where(used_row[None], gathered[r, p], 0.0).reshape(chips * padded, lanes)
            high, low = halves(values)
            return mm(inv_high[p], high) + mm(inv_high[p], low) + mm(inv_low[p], high)

        half = coarse(core)
        relay_copy(1 - core).wait_recv()
        partial[...] = (half + coarse(1 - core)).reshape(ny, padded, lanes)

        @pl.loop(1, ny)
        def _(i):
            other = lax.rem(b + i, ny)
            scatter_copy(partial.at[other, 0:modes], scattered.at[r, b, 0:modes], (a, other)).start()

        matched = live * y
        for f in range(4):
            @pl.when(exists[f])
            def _(f=f):
                face_copy(f, f).wait_recv()
            for piece in thirds(jnp.where(exists[f], face_recv[r, f], 0.0)):
                matched = matched + mm(piece, pick[f])
        v_ref[...] = matched

        scatter_copy(partial.at[0:ny - 1, 0:modes], scattered.at[r, 0:ny - 1, 0:modes], (partner, b)).wait_recv()
        solved = jnp.where(b == 0, partial[0], scattered[r, 0])
        for e in range(1, ny):
            solved = solved + jnp.where(b == e, partial[e], scattered[r, e])
        solved_send[...] = solved
        for f in range(4):
            @pl.when(exists[f])
            def _(f=f):
                solved_copy(f, f ^ 1).start()

        blocks = [jnp.where(used_row, solved, 0.0)]
        for f in range(4):
            @pl.when(exists[f])
            def _(f=f):
                solved_copy(f, f).wait_recv()
            blocks.append(jnp.where(used_row & exists[f], solved_recv[r, f], 0.0))
        high, low = halves(jnp.concatenate(blocks, axis=0))
        correction = dot_tn(high, mode_ext[...]) + dot_tn(low, mode_ext[...])
        out = v_ref[...] - correction[0:loads]

        for f in range(4):
            @pl.when(exists[f])
            def _(f=f):
                part_copy(f, f ^ 1).wait_send()
                face_copy(f, f ^ 1).wait_send()
                solved_copy(f, f ^ 1).wait_send()
        gather_copy(others, (partner, b)).wait_send()
        relay_copy(core).wait_send()
        scatter_copy(partial.at[0:ny - 1, 0:modes], scattered.at[r, 0:ny - 1, 0:modes], (partner, b)).wait_send()

        def advance(vector, which):
            y_ref[...] = mm(vector.astype(BF16), weights[which])

        @pl.when(r == 0)
        def _():
            res_ref[...] = out
            advance(out, 0)

        @pl.when(r == 1)
        def _():
            step = chebyshev[0][0] * out
            dir_ref[...] = step
            mult_ref[...] = step
            advance(step, 1)

        @pl.when(r == 2)
        def _():
            rest = res_ref[...] - out
            res_ref[...] = rest
            advance(rest, 0)

        @pl.when(r == 3)
        def _():
            step = chebyshev[1][0] * out + chebyshev[1][1] * dir_ref[...]
            mult_ref[...] = mult_ref[...] + step
            advance(step, 1)

        @pl.when(r == 4)
        def _():
            res_ref[...] = res_ref[...] - out

        return carry

    lax.fori_loop(0, ROUNDS, body, 0)


def local(nx, ny, load, dual_operator, dirichlet, modes, coarse_inverse, face_counts, partners):
    loads, slots = load.shape[2:]
    count = modes.shape[2]
    face = slots // 4
    face_pad = -(-face // 128) * 128
    padded = 16
    lanes = 128
    positions = lax.broadcasted_iota(jnp.int32, (4, face), 1)
    base = lax.broadcasted_iota(jnp.int32, (4, face), 0) * face_pad
    slot = jnp.where(positions < face_counts[0, 0][:, None], partners[0, 0] + base, -1)
    slot = slot.reshape(1, slots)
    vmem = pl.BlockSpec(memory_space=pltpu.VMEM)
    hbm = pl.BlockSpec(memory_space=pl.ANY)
    dma = pltpu.SemaphoreType.DMA
    multipliers, residual = pl.pallas_call(
        functools.partial(kernel, nx, ny),
        out_shape=(jax.ShapeDtypeStruct((loads, slots), F32),) * 2,
        in_specs=[vmem, vmem, vmem, hbm, hbm, hbm],
        out_specs=(vmem, vmem),
        scratch_shapes=[
            pltpu.VMEM((2, slots, slots), BF16),
            pltpu.VMEM((ny * count, nx * count), F32),
            pltpu.VMEM((4, face_pad, slots), BF16),
            pltpu.VMEM((5 * padded, slots), BF16),
            pltpu.VMEM((4, padded, face_pad), F32),
            pltpu.VMEM((4, padded, face_pad), F32),
            pltpu.VMEM((loads, slots), F32),
            pltpu.VMEM((loads, slots), F32),
            pltpu.VMEM((loads, slots), F32),
            pltpu.VMEM((2, ny * padded, nx // 2 * padded), BF16),
            pltpu.VMEM((2, ny * padded, nx // 2 * padded), BF16),
            pltpu.VMEM((4, loads, face_pad), F32),
            pltpu.VMEM((ROUNDS, 4, loads, face_pad), F32),
            pltpu.VMEM((5, padded, lanes), F32),
            pltpu.VMEM((ROUNDS, 4, padded, lanes), F32),
            pltpu.VMEM((ROUNDS, 2, nx // 2, padded, lanes), F32),
            pltpu.VMEM((ny, padded, lanes), F32),
            pltpu.VMEM((ROUNDS, ny, padded, lanes), F32),
            pltpu.VMEM((padded, lanes), F32),
            pltpu.VMEM((ROUNDS, 4, padded, lanes), F32),
            dma((3,)), dma((4,)), dma((4,)), dma((4,)), dma((ROUNDS, 4)),
            dma((4,)), dma((ROUNDS, 4)), dma, dma((ROUNDS,)), dma, dma((ROUNDS,)),
            dma, dma((ROUNDS,)), dma((4,)), dma((ROUNDS, 4)),
        ],
        compiler_params=pltpu.CompilerParams(
            collective_id=0, has_side_effects=True, vmem_limit_bytes=56 * 1024 * 1024),
    )(slot, load[0, 0], modes[0, 0], dual_operator[0, 0], dirichlet[0, 0], coarse_inverse[0, :, 0, :])
    return multipliers[None, None], residual[None, None]


def solution(mesh):
    nx, ny = mesh.shape["gx"], mesh.shape["gy"]
    return jax.shard_map(
        functools.partial(local, nx, ny),
        mesh=mesh,
        in_specs=(
            P("gx", "gy", None, None),
            P("gx", "gy", None, None),
            P("gx", "gy", None, None),
            P("gx", "gy", None, None),
            P("gx", None, "gy", None),
            P("gx", "gy", None),
            P("gx", "gy", None, None),
        ),
        out_specs=(P("gx", "gy", None, None), P("gx", "gy", None, None)),
        check_vma=False,
    )
```

```python
import functools

import jax
import jax.numpy as jnp
from jax import lax
from jax.experimental import pallas as pl
from jax.experimental.pallas import tpu as pltpu
from jax.sharding import PartitionSpec as P

MESH = pl.DeviceIdType.MESH
F32 = jnp.float32
BF16 = jnp.bfloat16
ROUNDS = 5
spectrum_low = 0.5
spectrum_high = 4.0


def chebyshev_coefficients():
    center = (spectrum_high + spectrum_low) / 2.0
    radius = (spectrum_high - spectrum_low) / 2.0
    center_ratio = center / radius
    factor_prev = 1.0 / center_ratio
    result = [(1.0 / center, 0.0)]
    factor = 1.0 / (2.0 * center_ratio - factor_prev)
    result.append((2.0 * factor / radius, factor * factor_prev))
    return result


def halves(x):
    high = x.astype(BF16)
    return high, (x - high.astype(F32)).astype(BF16)


def thirds(x):
    high = x.astype(BF16)
    rest = x - high.astype(F32)
    mid = rest.astype(BF16)
    return high, mid, (rest - mid.astype(F32)).astype(BF16)


def wrap_rows(x, loads, rows):
    spare = x.shape[1] - loads
    row = lax.bitwise_and(lax.broadcasted_iota(jnp.int32, x.shape, 0), 15)
    lane = lax.broadcasted_iota(jnp.int32, x.shape, 1)
    out = x
    for j in range(3):
        moved = pltpu.roll(pltpu.roll(x, loads - spare * j, 1), x.shape[0] - rows + 3 * j, 0)
        out = jnp.where((lane >= loads) & (row >= 3 * j) & (row < 3 * j + 3), moved, out)
    return out


def unwrap_rows(x, loads, rows):
    spare = x.shape[1] - loads
    row = lax.bitwise_and(lax.broadcasted_iota(jnp.int32, x.shape, 0), 15)
    lane = lax.broadcasted_iota(jnp.int32, x.shape, 1)
    out = jnp.where((row < rows) & (lane < loads), x, 0.0)
    for j in range(3):
        moved = pltpu.roll(pltpu.roll(x, spare * (j + 1), 1), rows - 3 * j, 0)
        here = (row >= rows) & (row < rows + 3) & (lane >= spare * j) & (lane < spare * (j + 1))
        out = jnp.where(here, moved, out)
    return out


def mm(a, b):
    return jnp.dot(a, b, preferred_element_type=F32)


def dot_nt(a, b):
    return lax.dot_general(a, b, (((1,), (1,)), ((), ())), preferred_element_type=F32)


def dot_tn(a, b):
    return lax.dot_general(a, b, (((0,), (0,)), ((), ())), preferred_element_type=F32)


def kernel(
    nx, ny,
    counts_hbm, partners_hbm, load_hbm, modes_hbm, dual_hbm, dirichlet_hbm, inverse_hbm,
    mult_ref, step_ref, res_ref, last_ref,
    counts_ref, partners_ref, modes_ref, x_ref, dm_high, dm_low,
    weights, inverse_raw, pick, mode_ext, mode_send, mode_recv,
    y_ref, v_ref, inv_high, inv_low,
    face_send, face_recv, part_send, near_recv, gathered,
    partial, across_recv, summed, along_recv, side_recv,
    local_sem, mode_ssem, mode_rsem, face_ssem, face_rsem, near_ssem, near_rsem,
    gather_ssem, gather_rsem, relay_ssem, relay_rsem,
    across_ssem, across_rsem, along_ssem, along_rsem, side_ssem, side_rsem,
):
    loads, slots = y_ref.shape
    modes = modes_ref.shape[0]
    face = slots // 4
    face_pad = face_send.shape[2]
    padded, lanes = gathered.shape[4:]
    depth = gathered.shape[2] + 1
    width = gathered.shape[3]
    height = along_recv.shape[1]
    length = ny // height
    chips = nx // 2
    a = lax.axis_index("gx")
    b = lax.axis_index("gy")
    core = lax.rem(a, 2)
    chip = lax.div(a, 2)
    layer = lax.div(chip, width)
    column = lax.rem(chip, width)
    far = lax.div(b, height)
    rise = lax.rem(b, height)

    def seat(z, y, c):
        return 2 * (z * width + y) + c

    next_column = (lax.rem(column + width - 1 + core, width), lax.rem(column + core, width))
    steps = sorted(range(1, width), key=lambda i: -min(i, width - i))
    partner = a + 1 - 2 * core
    exists = (a > 0, a < nx - 1, b > 0, b < ny - 1)
    neighbours = ((a - 1, b), (a + 1, b), (a, b - 1), (a, b + 1))

    def remote(src, dst, ssem, rsem, device):
        return pltpu.make_async_remote_copy(
            src_ref=src, dst_ref=dst, send_sem=ssem, recv_sem=rsem,
            device_id=device, device_id_type=MESH)

    copies = [pltpu.make_async_copy(src, dst, local_sem.at[i]) for i, (src, dst) in enumerate((
        (counts_hbm, counts_ref), (partners_hbm, partners_ref), (modes_hbm, modes_ref),
        (inverse_hbm.at[:, 0], inverse_raw), (load_hbm, y_ref),
        (dirichlet_hbm, weights.at[0]), (dual_hbm, weights.at[1])))]
    for c in copies:
        c.start()

    barrier = pltpu.get_barrier_semaphore()

    def greet(device):
        pl.semaphore_signal(barrier, inc=1, device_id=device, device_id_type=MESH)

    @pl.loop(1, depth)
    def _(i):
        greet((seat(lax.rem(layer + i, depth), column, core), b))

    @pl.loop(1, width)
    def _(i):
        greet((seat(layer, lax.rem(column + i, width), core), b))

    @pl.loop(0, depth)
    def _(z):
        greet((seat(z, next_column[0], 1 - core), b))
        greet((seat(z, next_column[1], 1 - core), b))

    for f in (2, 3):
        @pl.when(exists[f])
        def _(f=f):
            for i in range(1, depth):
                greet((seat(lax.rem(layer + i, depth), column, core), neighbours[f][1]))

    @pl.loop(1, ny)
    def _(i):
        greet((a, lax.rem(b + i, ny)))

    for f in (0, 1):
        @pl.when(exists[f])
        def _(f=f):
            for i in range(1, height):
                greet((neighbours[f][0], far * height + lax.rem(rise + i, height)))

    mode_send[...] = jnp.zeros_like(mode_send)
    copies[2].wait()
    wide = modes_ref[...].astype(F32)
    for f in range(4):
        mode_send[f, 0:modes, 0:face] = wide[:, f * face:(f + 1) * face]
    count = [e.astype(jnp.int32) for e in exists]
    pl.semaphore_wait(
        barrier, depth - 1 + width - 1 + 2 * depth + ny - 1
        + (depth - 1) * (count[2] + count[3]) + (height - 1) * (count[0] + count[1]))

    def mode_copy(f, g):
        return remote(mode_send.at[f], mode_recv.at[g], mode_ssem.at[f], mode_rsem.at[g], neighbours[f])

    for f in range(4):
        @pl.when(exists[f])
        def _(f=f):
            mode_copy(f, f ^ 1).start()

    face_send[...] = jnp.zeros_like(face_send)
    part_send[...] = jnp.zeros_like(part_send)
    partial[...] = jnp.zeros_like(partial)
    copies[0].wait()
    copies[1].wait()
    position = lax.broadcasted_iota(jnp.int32, (1, face), 1)
    slot = jnp.concatenate([
        jnp.where(position < counts_ref[:, f:f + 1], partners_ref[f:f + 1, :] + f * face_pad, -1)
        for f in range(4)], axis=1)
    live = (slot >= 0).astype(F32)
    for f in range(4):
        rows = lax.broadcasted_iota(jnp.int32, (face_pad, slots), 0) + f * face_pad
        pick[f] = (rows == slot).astype(F32).astype(BF16)
    own_modes = jnp.concatenate([wide * live, jnp.zeros((padded - modes, slots), F32)], axis=0)
    mode_ext[0:padded, :] = own_modes.astype(BF16)

    copies[3].wait()
    raw_high, raw_low = halves(inverse_raw[...])
    out_row = lax.broadcasted_iota(jnp.int32, (ny * padded, ny * modes), 0)
    in_row = lax.broadcasted_iota(jnp.int32, (ny * padded, ny * modes), 1)
    place = lax.bitwise_and(out_row, padded - 1)
    row_pick = ((lax.shift_right_logical(out_row, 4) * modes + place == in_row) & (place < modes))
    row_pick = row_pick.astype(F32).astype(BF16)
    raw_high = mm(row_pick, raw_high).astype(BF16)
    raw_low = mm(row_pick, raw_low).astype(BF16)
    for p in range(2):
        in_col = lax.broadcasted_iota(jnp.int32, (nx * modes, chips * padded), 0)
        out_col = lax.broadcasted_iota(jnp.int32, (nx * modes, chips * padded), 1)
        place = lax.bitwise_and(out_col, padded - 1)
        group = lax.shift_right_logical(out_col, 4)
        source = (2 * group + p) * modes + place
        col_pick = ((source == in_col) & (place < modes)).astype(F32).astype(BF16)
        inv_high[p] = mm(raw_high, col_pick).astype(BF16)
        inv_low[p] = mm(raw_low, col_pick).astype(BF16)

    for f in range(4):
        @pl.when(exists[f])
        def _(f=f):
            mode_copy(f, f).wait_recv()
        given = jnp.where(exists[f], mode_recv[f], 0.0).astype(BF16)
        mode_ext[(f + 1) * padded:(f + 2) * padded, :] = mm(given, pick[f]).astype(BF16)

    for f in range(4):
        @pl.when(exists[f])
        def _(f=f):
            mode_copy(f, f ^ 1).wait_send()

    packed = modes * loads // lanes

    def share(parts):
        blank = jnp.zeros((5 * padded, lanes - loads), F32)
        wide = wrap_rows(jnp.concatenate([parts, blank], axis=1), loads, packed)
        part_send[...] = wide.reshape(5, padded, lanes)

    copies[4].wait()
    high, low = halves(y_ref[...])
    share(dot_nt(mode_ext[...], high) + dot_nt(mode_ext[...], low))

    spare = lanes - loads
    lane = lax.broadcasted_iota(jnp.int32, (padded, lanes), 1)
    wide_lane = lax.broadcasted_iota(jnp.int32, (width * padded, lanes), 1)
    used_row = lax.broadcasted_iota(jnp.int32, (padded, lanes), 0) < modes
    chebyshev = chebyshev_coefficients()

    def body(r, carry):
        def face_copy(f, g):
            return remote(face_send.at[f], face_recv.at[r, g],
                          face_ssem.at[f], face_rsem.at[r, g], neighbours[f])

        def near_copy(f, spot, device):
            return remote(part_send.at[f, 0:packed], near_recv.at[r, spot, f if f == 0 else ((f - 1) ^ 1) + 1, 0:packed],
                          near_ssem.at[f], near_rsem.at[r, f if f == 0 else ((f - 1) ^ 1) + 1], device)

        def near_block(kind, n):
            block = near_recv.at[r, 0:n, kind, 0:packed]
            return remote(block, block, near_ssem.at[kind], near_rsem.at[r, kind], (partner, b))

        def gather_copy(block, device):
            return remote(block, block, gather_ssem, gather_rsem.at[r], device)

        def relay_copy(p):
            block = gathered.at[r, p, :, :, 0:modes]
            return remote(block, block, relay_ssem, relay_rsem.at[r], (partner, b))

        def across_copy(src, dst, device):
            return remote(src, dst, across_ssem, across_rsem.at[r], device)

        def along_copy(src, dst, device):
            return remote(src, dst, along_ssem, along_rsem.at[r], device)

        def side_copy(src, dst, side, device):
            return remote(src, dst, side_ssem.at[side], side_rsem.at[r, 1 - side], device)

        def side_block(side):
            block = side_recv.at[r, side, :, 0:packed]
            return remote(block, block, side_ssem.at[side], side_rsem.at[r, side], (partner, b))

        for f in (3, 2):
            @pl.when(exists[f])
            def _(f=f):
                for i in range(depth):
                    device = (seat(lax.rem(layer + i, depth), column, core), neighbours[f][1])
                    near_copy(f + 1, layer, device).start()
        for f in (0, 1):
            @pl.when(exists[f])
            def _(f=f):
                spot = lax.div(lax.div(neighbours[f][0], 2), width)
                for z in range(depth):
                    near_copy(f + 1, spot, (seat(z, next_column[f], 1 - core), b)).start()
        for i in range(1, depth):
            near_copy(0, layer, (seat(lax.rem(layer + i, depth), column, core), b)).start()
        @pl.when(r == 0)
        def _():
            copies[5].wait()
            copies[6].wait()
            for which in range(2):
                high, low = halves(dot_nt(mode_ext[...], weights[which]))
                dm_high[which] = high
                dm_low[which] = low

        @pl.when(r > 0)
        def _():
            y_ref[...] = mm(x_ref[...], weights[lax.rem(r + 1, 2)])

        y = y_ref[...]
        for f in range(4):
            face_send[f, :, 0:face] = y[:, f * face:(f + 1) * face]

        first = (column == 0) & (core == 0)
        final = (column == width - 1) & (core == 1)
        near_block(0, depth - 1).wait_recv()
        for kind, edge in ((1, first), (2, final)):
            @pl.when(edge)
            def _(kind=kind):
                near_block(kind, depth - 1).wait_recv()

            @pl.when(jnp.logical_not(edge))
            def _(kind=kind):
                near_block(kind, depth).wait_recv()
        for f in (2, 3):
            @pl.when(exists[f])
            def _(f=f):
                near_block(f + 1, depth).wait_recv()
        sums = []
        for z in range(depth):
            coeffs = jnp.where(layer == z, part_send[0], near_recv[r, z, 0])
            west, east = near_recv[r, z, 1], near_recv[r, z, 2]
            if z == 0:
                west = jnp.where(first, 0.0, west)
            if z == depth - 1:
                east = jnp.where(final, 0.0, east)
            coeffs = coeffs + (west + east)
            for f in (2, 3):
                coeffs = coeffs + jnp.where(exists[f], near_recv[r, z, f + 1], 0.0)
            sums.append(unwrap_rows(coeffs, loads, packed))
        for z in range(depth - 1):
            tail = pltpu.roll(sums[-1], loads - spare * z, 1)
            gathered[r, core, z, column] = jnp.where(lane < loads, sums[z], tail)
        mine = gathered.at[r, core, :, column, 0:modes]
        for i in steps:
            gather_copy(mine, (seat(layer, lax.rem(column + i, width), core), b)).start()

        for f in range(4):
            @pl.when(exists[f])
            def _(f=f):
                face_copy(f, f ^ 1).start()

        others = gathered.at[r, core, :, 0:width - 1, 0:modes]
        gather_copy(others, (partner, b)).wait_recv()
        relay_copy(core).start()

        def coarse(p):
            heads = [jnp.where(used_row[None], gathered[r, p, z], 0.0).reshape(width * padded, lanes)
                     for z in range(depth - 1)]
            last = pltpu.roll(heads[-1], lanes - spare, 1)
            for z in reversed(range(depth - 2)):
                last = jnp.where(wide_lane < spare * (z + 1), pltpu.roll(heads[z], spare * (z + 1), 1), last)
            values = jnp.concatenate(heads + [last], axis=0)
            high, low = halves(values)
            return mm(inv_high[p], high) + mm(inv_high[p], low) + mm(inv_low[p], high)

        half = coarse(core)
        relay_copy(1 - core).wait_recv()
        outcome = wrap_rows(half + coarse(1 - core), loads, packed)
        partial[1:ny + 1] = outcome.reshape(ny, padded, lanes)

        for i in range(1, length):
            other = lax.rem(far + i, length)
            across_copy(partial.at[pl.ds(height * other, height + 2), 0:packed],
                        across_recv.at[r, far, :, 0:packed], (a, other * height + rise)).start()
        across_all = across_recv.at[r, 0:length - 1, :, 0:packed]
        across_copy(across_all, across_all, (partner, b)).wait_recv()
        total = partial[pl.ds(height * far, height + 2)]
        for x in range(length):
            total = total + jnp.where(far == x, 0.0, across_recv[r, x])
        summed[...] = total
        for i in range(1, height):
            other = lax.rem(rise + i, height)
            along_copy(summed.at[pl.ds(other, 3), 0:packed], along_recv.at[r, rise, :, 0:packed],
                       (a, far * height + other)).start()
        for side in range(2):
            @pl.when(exists[side])
            def _(side=side):
                for i in range(height):
                    other = lax.rem(rise + height - i, height)
                    side_copy(summed.at[other + 1, 0:packed], side_recv.at[r, 1 - side, rise, 0:packed],
                              side, (neighbours[side][0], far * height + other)).start()

        matched = live * y
        for f in range(4):
            @pl.when(exists[f])
            def _(f=f):
                face_copy(f, f).wait_recv()
            for piece in thirds(jnp.where(exists[f], face_recv[r, f], 0.0)):
                matched = matched + mm(piece, pick[f])
        v_ref[...] = matched

        along_all = along_recv.at[r, 0:height - 1, :, 0:packed]
        along_copy(along_all, along_all, (partner, b)).wait_recv()
        trio = summed[pl.ds(rise, 3)]
        for z in range(height):
            trio = trio + jnp.where(rise == z, 0.0, along_recv[r, z])
        sides = []
        for side in range(2):
            @pl.when(exists[side])
            def _(side=side):
                side_block(side).wait_recv()
            sides.append(sum(side_recv[r, side, z] for z in range(height)))
        blocks = [trio[1]]
        for f, block in enumerate((sides[0], sides[1], trio[0], trio[2])):
            blocks.append(jnp.where(exists[f], block, 0.0))
        full = unwrap_rows(jnp.concatenate(blocks, axis=0), loads, packed)
        high, low = halves(full)
        correction = dot_tn(high, mode_ext[...]) + dot_tn(low, mode_ext[...])
        out = v_ref[...] - correction[0:loads]

        for f in range(4):
            @pl.when(exists[f])
            def _(f=f):
                near_block(f + 1, depth).wait_send()
                face_copy(f, f ^ 1).wait_send()
        for side in range(2):
            @pl.when(exists[side])
            def _(side=side):
                side_block(side).wait_send()
        near_block(0, depth - 1).wait_send()
        gather_copy(others, (partner, b)).wait_send()
        relay_copy(core).wait_send()
        across_copy(across_all, across_all, (partner, b)).wait_send()
        along_copy(along_all, along_all, (partner, b)).wait_send()

        def advance(vector, which):
            x = vector.astype(BF16)
            share(dot_nt(dm_high[which], x) + dot_nt(dm_low[which], x))
            x_ref[...] = x

        @pl.when(r == 0)
        def _():
            res_ref[...] = out
            advance(out, 0)

        @pl.when(r == 1)
        def _():
            step = chebyshev[0][0] * out
            mult_ref[...] = step
            advance(step, 1)

        @pl.when(r == 2)
        def _():
            rest = res_ref[...] - out
            res_ref[...] = rest
            advance(rest, 0)

        @pl.when(r == 3)
        def _():
            step = chebyshev[1][0] * out + chebyshev[1][1] * mult_ref[...]
            step_ref[...] = step
            advance(step, 1)

        @pl.when(r == 4)
        def _():
            last_ref[...] = out

        return carry

    lax.fori_loop(0, ROUNDS, body, 0)


def local(nx, ny, load, dual_operator, dirichlet, modes, coarse_inverse, face_counts, partners):
    loads, slots = load.shape[2:]
    count = modes.shape[2]
    face = slots // 4
    face_pad = -(-face // 128) * 128
    padded = 16
    lanes = 128
    depth = 4
    width = nx // 2 // depth
    height = 3 if ny % 3 == 0 else 2
    vmem = pl.BlockSpec(memory_space=pltpu.VMEM)
    hbm = pl.BlockSpec(memory_space=pltpu.HBM)
    dma = pltpu.SemaphoreType.DMA
    first, second, before, last = pl.pallas_call(
        functools.partial(kernel, nx, ny),
        out_shape=(jax.ShapeDtypeStruct((loads, slots), F32),) * 4,
        in_specs=[hbm] * 7,
        out_specs=(vmem,) * 4,
        scratch_shapes=[
            pltpu.VMEM((1, 4), jnp.int32),
            pltpu.VMEM((4, face), jnp.int32),
            pltpu.VMEM((count, slots), BF16),
            pltpu.VMEM((loads, slots), BF16),
            pltpu.VMEM((2, 5 * padded, slots), BF16),
            pltpu.VMEM((2, 5 * padded, slots), BF16),
            pltpu.VMEM((2, slots, slots), BF16),
            pltpu.VMEM((ny * count, nx * count), F32),
            pltpu.VMEM((4, face_pad, slots), BF16),
            pltpu.VMEM((5 * padded, slots), BF16),
            pltpu.VMEM((4, padded, face_pad), F32),
            pltpu.VMEM((4, padded, face_pad), F32),
            pltpu.VMEM((loads, slots), F32),
            pltpu.VMEM((loads, slots), F32),
            pltpu.VMEM((2, ny * padded, nx // 2 * padded), BF16),
            pltpu.VMEM((2, ny * padded, nx // 2 * padded), BF16),
            pltpu.VMEM((4, loads, face_pad), F32),
            pltpu.VMEM((ROUNDS, 4, loads, face_pad), F32),
            pltpu.VMEM((5, padded, lanes), F32),
            pltpu.VMEM((ROUNDS, depth, 5, padded, lanes), F32),
            pltpu.VMEM((ROUNDS, 2, depth - 1, width, padded, lanes), F32),
            pltpu.VMEM((ny + 2, padded, lanes), F32),
            pltpu.VMEM((ROUNDS, ny // height, height + 2, padded, lanes), F32),
            pltpu.VMEM((height + 2, padded, lanes), F32),
            pltpu.VMEM((ROUNDS, height, 3, padded, lanes), F32),
            pltpu.VMEM((ROUNDS, 2, height, padded, lanes), F32),
            dma((7,)), dma((4,)), dma((4,)), dma((4,)), dma((ROUNDS, 4)), dma((5,)), dma((ROUNDS, 5)),
            dma, dma((ROUNDS,)), dma, dma((ROUNDS,)),
            dma, dma((ROUNDS,)), dma, dma((ROUNDS,)), dma((2,)), dma((ROUNDS, 2)),
        ],
        compiler_params=pltpu.CompilerParams(
            collective_id=0, has_side_effects=True, vmem_limit_bytes=40 * 1024 * 1024),
    )(*(pltpu.with_memory_space_constraint(x, pltpu.HBM) for x in (
        face_counts[0], partners[0, 0], load[0, 0], modes[0, 0],
        dual_operator[0, 0], dirichlet[0, 0], coarse_inverse[0])))
    return (first + second)[None, None], (before - last)[None, None]


def solution(mesh):
    nx, ny = mesh.shape["gx"], mesh.shape["gy"]
    return jax.shard_map(
        functools.partial(local, nx, ny),
        mesh=mesh,
        in_specs=(
            P("gx", "gy", None, None),
            P("gx", "gy", None, None),
            P("gx", "gy", None, None),
            P("gx", "gy", None, None),
            P("gx", None, "gy", None),
            P("gx", "gy", None),
            P("gx", "gy", None, None),
        ),
        out_specs=(P("gx", "gy", None, None), P("gx", "gy", None, None)),
        check_vma=False,
    )
```
